32 devices in a mesh: row: 4 (over y, core), col: 8 (over z, x).
Axes of the slice: x: 2, y: 2, z: 4, core: 2. Of those that a mesh axis runs over, the one named last changes fastest.
Arguments:
- layer_input: bfloat16 [256, 8192], P('row', 'col'), may hold values from -36 to 36, as said below
- norm_gain: float32 [8192], P('col'), may hold values from 0.1 to 1.9
- w_gate: bfloat16 [8192, 14336], P('col', 'row'), may hold values from -0.09375 to 0.09375
- w_up: bfloat16 [8192, 14336], P('col', 'row'), may hold values from -0.09375 to 0.09375
- w_down: bfloat16 [14336, 8192], P('row', 'col'), may hold values from -0.09375 to 0.09375
- mask_gate: int32 [64, 112], P('col', 'row'), may hold values 0 or 1
- mask_up: int32 [64, 112], P('col', 'row'), may hold values 0 or 1
- mask_down: int32 [112, 64], P('row', 'col'), may hold values 0 or 1
- out_grad: bfloat16 [256, 8192], P('row', 'col'), may hold values from -6 to 6
Outputs:
- layer_out: bfloat16 [256, 8192], P('row', 'col')
- input_grad: bfloat16 [256, 8192], P('row', 'col')
- gain_grad: float32 [8192], P('col')
- gate_wgrad: bfloat16 [8192, 14336], P('col', 'row')
- up_wgrad: bfloat16 [8192, 14336], P('col', 'row')
- down_wgrad: bfloat16 [14336, 8192], P('row', 'col')
The draws below stay inside these ranges and needn't reach their ends.
Inputs may be any that keep to these rules, and one draw needn't show every extreme that they name: `layer_input`: the layer input's rows and features have scales that differ by up to a factor of ten.
All inputs are finite; a program needn't handle non-finite values. No bound on the sum of `mask_gate` or of `mask_up` or of `mask_down` on one device may be relied on, other than what follows from the above.
Results may differ from the reference program's by a relative error of at most 0.02.
Values may be sent and summed in bfloat16 or wider, within the bound.
A program may use at most 192 MiB of HBM per device.

```python
import math
import jax
import jax.numpy as jnp
from jax import lax

D = 8192
FF = 14336
BLK = 128
TOKENS = 256


def draw_layer_input(key, part):
    row_key = jax.random.fold_in(key, 11)
    col_key = jax.random.fold_in(key, 12)
    base_key = jax.random.fold_in(key, 13)
    row_scale = jnp.exp(jax.random.uniform(row_key, (TOKENS, 1), jnp.float32, math.log(0.3), math.log(3.0)))
    col_scale = jnp.exp(jax.random.uniform(col_key, (1, D), jnp.float32, math.log(0.3), math.log(3.0)))
    base = jax.random.truncated_normal(base_key, -4.0, 4.0, (TOKENS, D), jnp.float32)
    return (base * row_scale * col_scale).astype(jnp.bfloat16)


def place_ends(array, key, smallest, largest):
    longest = array.shape.index(max(array.shape))
    spots = []
    for shift in (0, 1):
        where = [jax.random.randint(jax.random.fold_in(key, axis), (), 0, length) for axis, length in enumerate(array.shape)]
        where[longest] = (where[longest] + shift) % array.shape[longest]
        spots.append(tuple(where))
    return array.at[spots[0]].set(smallest).at[spots[1]].set(largest)


def shard_levels(stream_key, shape, split, least, largest):
    def one(dim, blocks):
        draws = jax.random.uniform(jax.random.fold_in(jax.random.fold_in(stream_key, 6), dim), (blocks,), jnp.float32, least / len(split), largest / len(split))
        return jnp.repeat(jnp.exp(draws), shape[dim] // blocks).reshape((-1,) + (1,) * (len(shape) - dim - 1))

    gain = one(*split[0])
    for cut in split[1:]:
        gain = gain * one(*cut)
    return gain


def gaussian(rng, extent, scale, limit, pieces=(), held_as=jnp.bfloat16):
    factor_of = shard_levels(rng, extent, pieces, -0.22, 0.18) if pieces else 1.0
    drawn = jax.random.normal(rng, extent, jnp.float32) * scale * factor_of
    return jnp.minimum(jnp.maximum(drawn, -limit), limit).astype(held_as)


def setup_inputs(seed: int = 0) -> dict:
    splits = jax.random.split(jax.random.key(seed), 10)
    layer_input = draw_layer_input(jax.random.fold_in(splits[9], 71), 0)
    norm_gain = jnp.clip(1.0 + 0.18 * jax.random.normal(splits[1], (D,), jnp.float32), 0.1, 1.9)
    w_gate = gaussian(splits[2], (D, FF), (D // 2) ** -0.5, 0.09375, ((0, 8), (1, 4)))
    w_up = gaussian(splits[3], (D, FF), (D // 2) ** -0.5, 0.09375, ((0, 8), (1, 4)))
    w_down = gaussian(splits[4], (FF, D), (FF // 4) ** -0.5, 0.09375, ((0, 4), (1, 8)))
    mask_gate = place_ends((jax.random.randint(splits[5], (D // BLK, FF // BLK), 0, 2) < 1).astype(jnp.int32), jax.random.fold_in(splits[5], 1), 0, 1)
    mask_up = place_ends((jax.random.randint(splits[6], (D // BLK, FF // BLK), 0, 2) < 1).astype(jnp.int32), jax.random.fold_in(splits[6], 1), 0, 1)
    mask_down = place_ends((jax.random.randint(splits[7], (FF // BLK, D // BLK), 0, 2) < 1).astype(jnp.int32), jax.random.fold_in(splits[7], 1), 0, 1)
    out_grad = gaussian(splits[8], (TOKENS, D), 1.0, 6.0, ((0, 4), (1, 8)))
    return dict(layer_input=layer_input, norm_gain=norm_gain, w_gate=w_gate, w_up=w_up, w_down=w_down, mask_gate=mask_gate, mask_up=mask_up, mask_down=mask_down, out_grad=out_grad)


norm_eps = 1e-05

def apply_mask(weight, mask):
    block_rows, block_cols = mask.shape
    row_count, col_count = weight.shape
    blocks = weight.reshape(block_rows, row_count // block_rows, block_cols, col_count // block_cols)
    keep = mask.astype(weight.dtype)[:, None, :, None]
    return (blocks * keep).reshape(row_count, col_count)

def contract_rows(left, right):
    return lax.dot_general(left, right, (((0,), (0,)), ((), ())), preferred_element_type=jnp.float32)

def contract_cols(left, right):
    return lax.dot_general(left, right, (((1,), (1,)), ((), ())), preferred_element_type=jnp.float32)

def reference(layer_input, norm_gain, w_gate, w_up, w_down, mask_gate, mask_up, mask_down, out_grad):
    x_float = layer_input.astype(jnp.float32)
    scale = lax.rsqrt(lax.optimization_barrier(jnp.sum(x_float * x_float, axis=1)) / D + norm_eps)[:, None]
    normed = (x_float * scale * norm_gain[None, :]).astype(jnp.bfloat16)
    eff_gate = apply_mask(w_gate, mask_gate)
    eff_up = apply_mask(w_up, mask_up)
    eff_down = apply_mask(w_down, mask_down)
    gate = jnp.dot(normed, eff_gate, preferred_element_type=jnp.float32)
    up = jnp.dot(normed, eff_up, preferred_element_type=jnp.float32)
    act = (jax.nn.silu(gate) * up).astype(jnp.bfloat16)
    layer_out = (x_float + jnp.dot(act, eff_down, preferred_element_type=jnp.float32)).astype(jnp.bfloat16)
    act_grad = contract_cols(out_grad, eff_down)
    down_wgrad = apply_mask(contract_rows(act, out_grad), mask_down).astype(jnp.bfloat16)
    sig = jax.nn.sigmoid(gate)
    gate_grad = (act_grad * up * sig * (1.0 + gate * (1.0 - sig))).astype(jnp.bfloat16)
    up_grad = (act_grad * gate * sig).astype(jnp.bfloat16)
    gate_wgrad = apply_mask(contract_rows(normed, gate_grad), mask_gate).astype(jnp.bfloat16)
    up_wgrad = apply_mask(contract_rows(normed, up_grad), mask_up).astype(jnp.bfloat16)
    normed_grad = contract_cols(gate_grad, eff_gate) + contract_cols(up_grad, eff_up)
    gain_grad = lax.optimization_barrier(jnp.sum(normed_grad * x_float * scale, axis=0))
    dots = lax.optimization_barrier(jnp.sum(normed_grad * norm_gain[None, :] * x_float, axis=1))[:, None]
    input_grad = (out_grad.astype(jnp.float32) + scale * norm_gain[None, :] * normed_grad - x_float * scale * scale * scale * dots / D).astype(jnp.bfloat16)
    return (layer_out, input_grad, gain_grad, gate_wgrad, up_wgrad, down_wgrad)
```

```python
import functools

import jax
import jax.numpy as jnp
from jax import lax
from jax.experimental import pallas as pl
from jax.experimental.pallas import tpu as pltpu
from jax.sharding import PartitionSpec as P

BLK = 128
LANES = 128
MESH = pl.DeviceIdType.MESH
F32 = jnp.float32
BF16 = jnp.bfloat16
norm_eps = 1e-05


def dot_nn(left, right):
    return lax.dot_general(left, right, (((1,), (0,)), ((), ())), preferred_element_type=F32)


def dot_nt(left, right):
    return lax.dot_general(left, right, (((1,), (1,)), ((), ())), preferred_element_type=F32)


def dot_tn(left, right):
    return lax.dot_general(left, right, (((0,), (0,)), ((), ())), preferred_element_type=F32)


def chunk_width(hidden):
    for width in (512, 256, 128):
        if hidden % width == 0:
            return width
    return hidden


def layer_kernel(
    R, NZ, NX, width, total_width,
    x_ref, gain_ref, og_ref, mg_ref, mu_ref, md_ref, wg_hbm, wu_hbm, wd_hbm,
    out_ref, ig_ref, gg_out, act_all, gg_all, ug_all, nm_out, og_out,
    wg, wu, wd, nm_all, og_all, sq_mine, sq_all, part_a, part_g, xr_a, xr_g,
    red_a, red_g, zr_a, zr_g, ag, acc_d, acc_n, fin_s, fin_r, gn_mine, gn_all,
    dt_mine, dt_all,
    w_sem, og_s, og_r, nm_s, nm_r, sq_s, sq_r, xa_s, xa_r, xg_s, xg_r,
    za_s, za_r, zg_s, zg_r, agz_s, agz_r, agx_s, agx_r, fin_ss, fin_rs,
    gn_s, gn_r, dt_s, dt_r, loc_s,
):
    C = NZ * NX
    row = lax.axis_index("row")
    col = lax.axis_index("col")
    mz = col // NX
    mx = lax.rem(col, NX)
    rows, feats = x_ref.shape
    hidden = wg.shape[1]
    n = hidden // width
    T = part_a.shape[3]
    per = width // BLK

    def rpeer(k):
        return lax.rem(row + k, R)

    def cpeer(k):
        return lax.rem(col + k, C)

    def xpeer(k):
        return lax.rem(mx + k, NX)

    def zpeer(k):
        return lax.rem(mz + k, NZ)

    def remote(src, dst, ssem, rsem, dev):
        return pltpu.make_async_remote_copy(
            src_ref=src, dst_ref=dst, send_sem=ssem, recv_sem=rsem,
            device_id=dev, device_id_type=MESH,
        )

    barrier = pltpu.get_barrier_semaphore()
    for k in range(1, R):
        pl.semaphore_signal(barrier, inc=1, device_id=(rpeer(k), col), device_id_type=MESH)
    for k in range(1, C):
        pl.semaphore_signal(barrier, inc=1, device_id=(row, cpeer(k)), device_id_type=MESH)
    loads = [
        pltpu.make_async_copy(src, dst, w_sem.at[i])
        for i, (src, dst) in enumerate(((wd_hbm, wd), (wg_hbm, wg), (wu_hbm, wu)))
    ]
    for load in loads:
        load.start()
    pl.semaphore_wait(barrier, R - 1 + C - 1)

    def og_copy(src, dev):
        return remote(og_ref, og_all.at[src], og_s.at[dev], og_r.at[src], (dev, col))

    for k in range(1, R):
        og_copy(row, rpeer(k)).start()
    own_og = pltpu.make_async_copy(og_ref, og_all.at[row], loc_s.at[0])
    own_og.start()

    x = x_ref[...].astype(F32)
    tok = lax.broadcasted_iota(jnp.int32, (rows, LANES), 0)
    lane = lax.broadcasted_iota(jnp.int32, (rows, LANES), 1)
    diag = tok == lane

    def to_lanes(column):
        return jnp.sum(jnp.where(diag, column, 0.0), axis=0, keepdims=True)

    def to_column(line):
        return jnp.sum(jnp.where(diag, line, 0.0), axis=1, keepdims=True)

    sq_mine[...] = to_lanes(jnp.sum(x * x, axis=1, keepdims=True))

    def sq_copy(src, dev):
        return remote(sq_mine, sq_all.at[src], sq_s.at[dev], sq_r.at[src], (row, dev))

    for k in range(1, C):
        sq_copy(col, cpeer(k)).start()

    loads[0].wait()
    own_og.wait()
    for k in range(1, R):
        og_copy(rpeer(k), rpeer(k)).wait_recv()

    def xa_copy(j, src, dev):
        return remote(
            part_a.at[j, dev], xr_a.at[j, src], xa_s.at[j, dev], xa_r.at[j, src],
            (row, mz * NX + dev),
        )

    def xg_copy(j, src, dev):
        return remote(
            part_g.at[j, dev], xr_g.at[j, src], xg_s.at[j, dev], xg_r.at[j, src],
            (row, mz * NX + dev),
        )

    def a_part(j, carry):
        base = pl.multiple_of(j * width, width)
        for r in range(per):
            at = pl.ds(pl.multiple_of(base + r * BLK, BLK), BLK)
            wd[at, :] = wd[at, :] * md_ref[j * per + r].astype(BF16)
        a = dot_nt(
            og_all[...].reshape(R * rows, feats), wd[pl.ds(base, width), :]
        ).astype(BF16)
        for z in range(NZ):
            for xx in range(NX):
                c = z * NX + xx
                part_a[j, xx, z] = a[c * T : (c + 1) * T]
        for k in range(1, NX):
            xa_copy(j, mx, xpeer(k)).start()
        return carry

    lax.fori_loop(0, n, a_part, 0)

    sq_all[col] = sq_mine[...]
    for k in range(1, C):
        sq_copy(cpeer(k), cpeer(k)).wait_recv()
    total = sq_all[0]
    for c in range(1, C):
        total = total + sq_all[c]
    scale = lax.rsqrt(to_column(total) / total_width + norm_eps)
    gain = gain_ref[...]
    nm_all[row] = (x * scale * gain).astype(BF16)

    def nm_copy(src, dev):
        return remote(
            nm_all.at[src], nm_all.at[src], nm_s.at[dev], nm_r.at[src], (dev, col)
        )

    for k in range(1, R):
        nm_copy(row, rpeer(k)).start()
    loads[1].wait()
    loads[2].wait()

    def mask_columns(j, carry):
        cols = pl.ds(pl.multiple_of(j * width, width), width)
        for r in range(feats // BLK):
            at = slice(r * BLK, (r + 1) * BLK)
            wg[at, cols] = wg[at, cols] * mg_ref[r, :, cols].astype(BF16)
            wu[at, cols] = wu[at, cols] * mu_ref[r, :, cols].astype(BF16)
        return carry

    lax.fori_loop(0, n, mask_columns, 0)
    for k in range(1, R):
        nm_copy(rpeer(k), rpeer(k)).wait_recv()

    def g_part(j, carry):
        cols = pl.ds(pl.multiple_of(j * width, width), width)
        nm = nm_all[...].reshape(R * rows, feats)
        for which, w in enumerate((wg, wu)):
            p = dot_nn(nm, w[:, cols]).astype(BF16)
            for z in range(NZ):
                for xx in range(NX):
                    c = z * NX + xx
                    part_g[j, xx, z, which] = p[c * T : (c + 1) * T]
        for k in range(1, NX):
            xg_copy(j, mx, xpeer(k)).start()
        return carry

    lax.fori_loop(0, n, g_part, 0)

    def za_copy(j, src, dev):
        return remote(
            red_a.at[j, dev], zr_a.at[j, src], za_s.at[j, dev], za_r.at[j, src],
            (row, dev * NX + mx),
        )

    def zg_copy(j, src, dev):
        return remote(
            red_g.at[j, dev], zr_g.at[j, src], zg_s.at[j, dev], zg_r.at[j, src],
            (row, dev * NX + mx),
        )

    def a_sum(j, carry):
        for k in range(1, NX):
            xa_copy(j, xpeer(k), xpeer(k)).wait_recv()
        s = part_a[j, mx].astype(F32)
        for k in range(1, NX):
            s = s + xr_a[j, xpeer(k)].astype(F32)
        red_a[j] = s.astype(BF16)
        for k in range(1, NZ):
            za_copy(j, mz, zpeer(k)).start()
        return carry

    lax.fori_loop(0, n, a_sum, 0)

    def agz_copy(j, src, dev):
        return remote(
            ag.at[j, mx, src], ag.at[j, mx, src], agz_s.at[j, dev], agz_r.at[j, src],
            (row, dev * NX + mx),
        )

    def agx_copy(j, src, dev):
        return remote(
            ag.at[j, src], ag.at[j, src], agx_s.at[j, dev], agx_r.at[j, src],
            (row, mz * NX + dev),
        )

    def g_sum(j):
        for k in range(1, NX):
            xg_copy(j, xpeer(k), xpeer(k)).wait_recv()
        for z in range(NZ):
            s = part_g[j, mx, z].astype(F32)
            for k in range(1, NX):
                s = s + xr_g[j, xpeer(k), z].astype(F32)
            red_g[j, z] = s.astype(BF16)
        for k in range(1, NZ):
            zg_copy(j, mz, zpeer(k)).start()

    def pointwise(j):
        for k in range(1, NZ):
            za_copy(j, zpeer(k), zpeer(k)).wait_recv()
            zg_copy(j, zpeer(k), zpeer(k)).wait_recv()
        da = red_a[j, mz].astype(F32)
        gate = red_g[j, mz, 0].astype(F32)
        up = red_g[j, mz, 1].astype(F32)
        for k in range(1, NZ):
            zp = zpeer(k)
            da = da + zr_a[j, zp].astype(F32)
            gate = gate + zr_g[j, zp, 0].astype(F32)
            up = up + zr_g[j, zp, 1].astype(F32)
        sig = jax.nn.sigmoid(gate)
        ag[j, mx, mz, 0] = (gate * sig * up).astype(BF16)
        ag[j, mx, mz, 1] = (da * up * sig * (1.0 + gate * (1.0 - sig))).astype(BF16)
        ag[j, mx, mz, 2] = (da * gate * sig).astype(BF16)
        for k in range(1, NZ):
            agz_copy(j, mz, zpeer(k)).start()

    def forward_x(j):
        for k in range(1, NZ):
            agz_copy(j, zpeer(k), zpeer(k)).wait_recv()
        for k in range(1, NX):
            agx_copy(j, mx, xpeer(k)).start()

    def exchange(s, carry):
        @pl.when(s < n)
        def _():
            g_sum(s)

        @pl.when(jnp.logical_and(s >= 1, s < n + 1))
        def _():
            pointwise(s - 1)

        @pl.when(s >= 2)
        def _():
            forward_x(s - 2)

        return carry

    lax.fori_loop(0, n + 2, exchange, 0)

    acc_d[...] = jnp.zeros_like(acc_d)
    acc_n[...] = jnp.zeros_like(acc_n)

    def products(j, carry):
        for k in range(1, NX):
            agx_copy(j, xpeer(k), xpeer(k)).wait_recv()
        cols = pl.ds(pl.multiple_of(j * width, width), width)

        def tokens(which):
            return jnp.concatenate(
                [ag[j, c % NX, c // NX, which] for c in range(C)], axis=0
            )

        act, gg, ug = tokens(0), tokens(1), tokens(2)
        act_all[:, cols] = act
        gg_all[:, cols] = gg
        ug_all[:, cols] = ug
        acc_d[...] += dot_nn(act, wd[cols, :])
        acc_n[...] += dot_nt(gg, wg[:, cols]) + dot_nt(ug, wu[:, cols])
        return carry

    lax.fori_loop(0, n, products, 0)

    for r in range(R):
        at = slice(r * rows, (r + 1) * rows)
        fin_s[r, 0] = acc_d[at, :].astype(BF16)
        fin_s[r, 1] = acc_n[at, :].astype(BF16)

    def fin_copy(src, dev):
        return remote(
            fin_s.at[dev], fin_r.at[src], fin_ss.at[dev], fin_rs.at[src], (dev, col)
        )

    for k in range(1, R):
        fin_copy(row, rpeer(k)).start()
    nm_out[...] = nm_all[...].reshape(R * rows, feats)
    og_out[...] = og_all[...].reshape(R * rows, feats)
    for k in range(1, R):
        fin_copy(rpeer(k), rpeer(k)).wait_recv()
    down = fin_s[row, 0].astype(F32)
    ngrad = fin_s[row, 1].astype(F32)
    for k in range(1, R):
        down = down + fin_r[rpeer(k), 0].astype(F32)
        ngrad = ngrad + fin_r[rpeer(k), 1].astype(F32)
    x = x_ref[...].astype(F32)
    dt_mine[...] = to_lanes(jnp.sum(ngrad * gain * x, axis=1, keepdims=True))
    gn_mine[...] = jnp.sum(ngrad * x * scale, axis=0, keepdims=True)

    def dt_copy(src, dev):
        return remote(dt_mine, dt_all.at[src], dt_s.at[dev], dt_r.at[src], (row, dev))

    def gn_copy(src, dev):
        return remote(gn_mine, gn_all.at[src], gn_s.at[dev], gn_r.at[src], (dev, col))

    for k in range(1, C):
        dt_copy(col, cpeer(k)).start()
    for k in range(1, R):
        gn_copy(row, rpeer(k)).start()
    dt_all[col] = dt_mine[...]
    gn_all[row] = gn_mine[...]
    out_ref[...] = (x + down).astype(BF16)
    for k in range(1, C):
        dt_copy(cpeer(k), cpeer(k)).wait_recv()
    dots = dt_all[0]
    for c in range(1, C):
        dots = dots + dt_all[c]
    dots = to_column(dots)
    ig_ref[...] = (
        og_ref[...].astype(F32)
        + scale * gain * ngrad
        - x * scale * scale * scale * dots / total_width
    ).astype(BF16)
    for k in range(1, R):
        gn_copy(rpeer(k), rpeer(k)).wait_recv()
    gain_sum = gn_all[0]
    for r in range(1, R):
        gain_sum = gain_sum + gn_all[r]
    gg_out[...] = gain_sum

    for k in range(1, R):
        og_copy(row, rpeer(k)).wait_send()
        nm_copy(row, rpeer(k)).wait_send()
        fin_copy(row, rpeer(k)).wait_send()
        gn_copy(row, rpeer(k)).wait_send()
    for k in range(1, C):
        sq_copy(col, cpeer(k)).wait_send()
        dt_copy(col, cpeer(k)).wait_send()

    def drain(j, carry):
        for k in range(1, NX):
            xa_copy(j, mx, xpeer(k)).wait_send()
            xg_copy(j, mx, xpeer(k)).wait_send()
            agx_copy(j, mx, xpeer(k)).wait_send()
        for k in range(1, NZ):
            za_copy(j, mz, zpeer(k)).wait_send()
            zg_copy(j, mz, zpeer(k)).wait_send()
            agz_copy(j, mz, zpeer(k)).wait_send()
        return carry

    lax.fori_loop(0, n, drain, 0)


def wgrad_kernel(per, nm_ref, og_ref, act_ref, gg_ref, ug_ref, mg_ref, mu_ref, md_ref,
                 gw_ref, uw_ref, dw_ref):
    feats = nm_ref.shape[1]
    for src, mask, dst in ((gg_ref, mg_ref, gw_ref), (ug_ref, mu_ref, uw_ref)):
        w = dot_tn(nm_ref[...], src[...])
        for r in range(feats // BLK):
            at = slice(r * BLK, (r + 1) * BLK)
            dst[at, :] = (w[at, :] * mask[r]).astype(BF16)
    w = dot_tn(act_ref[...], og_ref[...])
    for r in range(per):
        at = slice(r * BLK, (r + 1) * BLK)
        dw_ref[at, :] = (w[at, :] * md_ref[r]).astype(BF16)


def shards(R, C, layer_input, norm_gain, w_gate, w_up, w_down,
           mask_gate, mask_up, mask_down, out_grad):
    rows, feats = layer_input.shape
    hidden = w_gate.shape[1]
    tokens = rows * R
    T = tokens // C
    NX = 1
    while (2 * NX) * (2 * NX) <= C:
        NX *= 2
    NZ = C // NX
    width = chunk_width(hidden)
    n = hidden // width
    per = width // BLK
    wide_gate = jnp.repeat(mask_gate.astype(F32), BLK, axis=1)[:, None, :]
    wide_up = jnp.repeat(mask_up.astype(F32), BLK, axis=1)[:, None, :]
    wide_down = jnp.repeat(mask_down.astype(F32), BLK, axis=1)[:, None, :]
    vm = pl.BlockSpec(memory_space=pltpu.VMEM)
    hbm = pl.BlockSpec(memory_space=pl.ANY)
    dma = pltpu.SemaphoreType.DMA
    V = pltpu.VMEM
    out_shapes = (
        ((rows, feats), BF16), ((rows, feats), BF16), ((1, feats), F32),
        ((tokens, hidden), BF16), ((tokens, hidden), BF16), ((tokens, hidden), BF16),
        ((tokens, feats), BF16), ((tokens, feats), BF16),
    )
    scratch = [
        V((feats, hidden), BF16), V((feats, hidden), BF16), V((hidden, feats), BF16),
        V((R, rows, feats), BF16), V((R, rows, feats), BF16),
        V((1, LANES), F32), V((C, 1, LANES), F32),
        V((n, NX, NZ, T, width), BF16), V((n, NX, NZ, 2, T, width), BF16),
        V((n, NX, NZ, T, width), BF16), V((n, NX, NZ, 2, T, width), BF16),
        V((n, NZ, T, width), BF16), V((n, NZ, 2, T, width), BF16),
        V((n, NZ, T, width), BF16), V((n, NZ, 2, T, width), BF16),
        V((n, NX, NZ, 3, T, width), BF16),
        V((tokens, feats), F32), V((tokens, feats), F32),
        V((R, 2, rows, feats), BF16), V((R, 2, rows, feats), BF16),
        V((1, feats), F32), V((R, 1, feats), F32),
        V((1, LANES), F32), V((C, 1, LANES), F32),
        dma((3,)),
        dma((R,)), dma((R,)), dma((R,)), dma((R,)), dma((C,)), dma((C,)),
        dma((n, NX)), dma((n, NX)), dma((n, NX)), dma((n, NX)),
        dma((n, NZ)), dma((n, NZ)), dma((n, NZ)), dma((n, NZ)),
        dma((n, NZ)), dma((n, NZ)), dma((n, NX)), dma((n, NX)),
        dma((R,)), dma((R,)), dma((R,)), dma((R,)), dma((C,)), dma((C,)),
        dma((1,)),
    ]
    layer_out, input_grad, gain_grad, act, gg, ug, nm, og = pl.pallas_call(
        functools.partial(layer_kernel, R, NZ, NX, width, float(feats * C)),
        out_shape=tuple(jax.ShapeDtypeStruct(s, t) for s, t in out_shapes),
        in_specs=[vm] * 6 + [hbm] * 3,
        out_specs=tuple([vm] * 8),
        scratch_shapes=scratch,
        compiler_params=pltpu.CompilerParams(
            collective_id=0, has_side_effects=True, vmem_limit_bytes=67043328
        ),
    )(layer_input, norm_gain[None, :], out_grad, wide_gate, wide_up, wide_down,
      w_gate, w_up, w_down)

    whole = lambda j: (0, 0)
    gate_wgrad, up_wgrad, down_wgrad = pl.pallas_call(
        functools.partial(wgrad_kernel, per),
        grid=(n,),
        out_shape=(
            jax.ShapeDtypeStruct((feats, hidden), BF16),
            jax.ShapeDtypeStruct((feats, hidden), BF16),
            jax.ShapeDtypeStruct((hidden, feats), BF16),
        ),
        in_specs=[
            pl.BlockSpec((tokens, feats), whole),
            pl.BlockSpec((tokens, feats), whole),
            pl.BlockSpec((tokens, width), lambda j: (0, j)),
            pl.BlockSpec((tokens, width), lambda j: (0, j)),
            pl.BlockSpec((tokens, width), lambda j: (0, j)),
            pl.BlockSpec((feats // BLK, 1, width), lambda j: (0, 0, j)),
            pl.BlockSpec((feats // BLK, 1, width), lambda j: (0, 0, j)),
            pl.BlockSpec((per, 1, feats), lambda j: (j, 0, 0)),
        ],
        out_specs=(
            pl.BlockSpec((feats, width), lambda j: (0, j)),
            pl.BlockSpec((feats, width), lambda j: (0, j)),
            pl.BlockSpec((width, feats), lambda j: (j, 0)),
        ),
        compiler_params=pltpu.CompilerParams(vmem_limit_bytes=40 * 1024 * 1024),
    )(nm, og, act, gg, ug, wide_gate, wide_up, wide_down)
    return (layer_out, input_grad, gain_grad[0], gate_wgrad, up_wgrad, down_wgrad)


def solution(mesh):
    placed = (
        P("row", "col"),
        P("col"),
        P("col", "row"),
        P("col", "row"),
        P("row", "col"),
        P("col", "row"),
        P("col", "row"),
        P("row", "col"),
        P("row", "col"),
    )
    return jax.shard_map(
        functools.partial(shards, mesh.shape["row"], mesh.shape["col"]),
        mesh=mesh,
        in_specs=placed,
        out_specs=(
            P("row", "col"),
            P("row", "col"),
            P("col"),
            P("col", "row"),
            P("col", "row"),
            P("row", "col"),
        ),
        check_vma=False,
    )
```

```python
import functools

import jax
import jax.numpy as jnp
from jax import lax
from jax.experimental import pallas as pl
from jax.experimental.pallas import tpu as pltpu
from jax.sharding import PartitionSpec as P

BLK = 128
LANES = 128
MESH = pl.DeviceIdType.MESH
F32 = jnp.float32
BF16 = jnp.bfloat16
norm_eps = 1e-05


def dot_nn(left, right):
    return lax.dot_general(left, right, (((1,), (0,)), ((), ())), preferred_element_type=F32)


def dot_nt(left, right):
    return lax.dot_general(left, right, (((1,), (1,)), ((), ())), preferred_element_type=F32)


def dot_tn(left, right):
    return lax.dot_general(left, right, (((0,), (0,)), ((), ())), preferred_element_type=F32)


def chunk_width(hidden):
    for width in (512, 256, 128):
        if hidden % width == 0:
            return width
    return hidden


def layer_kernel(
    R, NZ, NX, width, total_width,
    x_ref, gain_ref, og_ref, mg_ref, mu_ref, md_ref, wg_hbm, wu_hbm, wd_hbm,
    out_ref, ig_ref, gg_out, act_all, gg_all, ug_all, nm_out, og_out,
    wg, wu, wd, nm_all, og_all, sq_mine, sq_all, part_a, part_g, xr_a, xr_g,
    red_a, red_g, zr_a, zr_g, cz_a, cz_g, da_sum, gu_sum, ag, acc_d, acc_n, fin_s, fin_r, gn_mine, gn_all,
    dt_mine, dt_all,
    w_sem, og_s, og_r, nm_s, nm_r, sq_s, sq_r, xa_s, xa_r, xg_s, xg_r,
    za_s, za_r, zg_s, zg_r, ca_r, cg_r, agz_s, agz_r, agf_s, agx_s, agx_r, fin_ss, fin_rs,
    gn_s, gn_r, dt_s, dt_r, loc_s,
):
    C = NZ * NX
    row = lax.axis_index("row")
    col = lax.axis_index("col")
    mz = col // NX
    mx = lax.rem(col, NX)
    rows, feats = x_ref.shape
    hidden = wg.shape[1]
    n = hidden // width
    T = part_a.shape[3]
    per = width // BLK

    def rpeer(k):
        return lax.rem(row + k, R)

    def cpeer(k):
        return lax.rem(col + k, C)

    def xpeer(k):
        return lax.rem(mx + k, NX)

    def zpeer(k):
        return lax.rem(mz + k, NZ)

    def remote(src, dst, ssem, rsem, dev):
        return pltpu.make_async_remote_copy(
            src_ref=src, dst_ref=dst, send_sem=ssem, recv_sem=rsem,
            device_id=dev, device_id_type=MESH,
        )

    barrier = pltpu.get_barrier_semaphore()
    for k in range(1, R):
        pl.semaphore_signal(barrier, inc=1, device_id=(rpeer(k), col), device_id_type=MESH)
    for k in range(1, C):
        pl.semaphore_signal(barrier, inc=1, device_id=(row, cpeer(k)), device_id_type=MESH)
    loads = [
        pltpu.make_async_copy(src, dst, w_sem.at[i])
        for i, (src, dst) in enumerate(((wd_hbm, wd), (wg_hbm, wg), (wu_hbm, wu)))
    ]
    for load in loads:
        load.start()
    pl.semaphore_wait(barrier, R - 1 + C - 1)

    def og_copy(src, dev):
        return remote(og_ref, og_all.at[src], og_s.at[dev], og_r.at[src], (dev, col))

    for k in range(1, R):
        og_copy(row, rpeer(k)).start()
    own_og = pltpu.make_async_copy(og_ref, og_all.at[row], loc_s.at[0])
    own_og.start()

    x = x_ref[...].astype(F32)
    tok = lax.broadcasted_iota(jnp.int32, (rows, LANES), 0)
    lane = lax.broadcasted_iota(jnp.int32, (rows, LANES), 1)
    diag = tok == lane

    def to_lanes(column):
        return jnp.sum(jnp.where(diag, column, 0.0), axis=0, keepdims=True)

    def to_column(line):
        return jnp.sum(jnp.where(diag, line, 0.0), axis=1, keepdims=True)

    sq_mine[...] = to_lanes(jnp.sum(x * x, axis=1, keepdims=True))

    def sq_copy(src, dev):
        return remote(sq_mine, sq_all.at[src], sq_s.at[dev], sq_r.at[src], (row, dev))

    for k in range(1, C):
        sq_copy(col, cpeer(k)).start()

    loads[0].wait()
    own_og.wait()
    for k in range(1, R):
        og_copy(rpeer(k), rpeer(k)).wait_recv()

    def xa_copy(j, src, dev):
        return remote(
            part_a.at[j, dev], xr_a.at[j, src], xa_s.at[j, dev], xa_r.at[j, src],
            (row, mz * NX + dev),
        )

    def xg_copy(j, src, dev):
        return remote(
            part_g.at[j, dev], xr_g.at[j, src], xg_s.at[j, dev], xg_r.at[j, src],
            (row, mz * NX + dev),
        )

    def a_part(j, carry):
        base = pl.multiple_of(j * width, width)
        for r in range(per):
            at = pl.ds(pl.multiple_of(base + r * BLK, BLK), BLK)
            wd[at, :] = wd[at, :] * md_ref[j * per + r].astype(BF16)
        a = dot_nt(
            og_all[...].reshape(R * rows, feats), wd[pl.ds(base, width), :]
        ).astype(BF16)
        for z in range(NZ):
            for xx in range(NX):
                c = z * NX + xx
                part_a[j, xx, z] = a[c * T : (c + 1) * T]
        for k in range(1, NX):
            xa_copy(j, mx, xpeer(k)).start()
        return carry

    lax.fori_loop(0, n, a_part, 0)

    sq_all[col] = sq_mine[...]
    for k in range(1, C):
        sq_copy(cpeer(k), cpeer(k)).wait_recv()
    total = sq_all[0]
    for c in range(1, C):
        total = total + sq_all[c]
    scale = lax.rsqrt(to_column(total) / total_width + norm_eps)
    gain = gain_ref[...]
    nm_all[row] = (x * scale * gain).astype(BF16)

    def nm_copy(src, dev):
        return remote(
            nm_all.at[src], nm_all.at[src], nm_s.at[dev], nm_r.at[src], (dev, col)
        )

    for k in range(1, R):
        nm_copy(row, rpeer(k)).start()
    loads[1].wait()
    loads[2].wait()

    def mask_columns(j, carry):
        cols = pl.ds(pl.multiple_of(j * width, width), width)
        for r in range(feats // BLK):
            at = slice(r * BLK, (r + 1) * BLK)
            wg[at, cols] = wg[at, cols] * mg_ref[r, :, cols].astype(BF16)
            wu[at, cols] = wu[at, cols] * mu_ref[r, :, cols].astype(BF16)
        return carry

    lax.fori_loop(0, n, mask_columns, 0)
    for k in range(1, R):
        nm_copy(rpeer(k), rpeer(k)).wait_recv()

    def g_part(j, carry):
        cols = pl.ds(pl.multiple_of(j * width, width), width)
        nm = nm_all[...].reshape(R * rows, feats)
        for which, w in enumerate((wg, wu)):
            p = dot_nn(nm, w[:, cols]).astype(BF16)
            for z in range(NZ):
                for xx in range(NX):
                    c = z * NX + xx
                    part_g[j, xx, z, which] = p[c * T : (c + 1) * T]
        for k in range(1, NX):
            xg_copy(j, mx, xpeer(k)).start()
        return carry

    lax.fori_loop(0, n, g_part, 0)

    def inside(z):
        return jnp.logical_and(z >= 0, z < NZ)

    def outside(z):
        return jnp.logical_or(z < 0, z >= NZ)

    kinds = ((red_a, zr_a, cz_a, za_s, za_r, ca_r), (red_g, zr_g, cz_g, zg_s, zg_r, cg_r))

    def z_near(kind, j, t, src):
        red, zr, _, ssem, rsem, _ = kind
        return remote(
            red.at[j, t], zr.at[j, src], ssem.at[j, t], rsem.at[j, src], (row, t * NX + mx)
        )

    def z_chain(kind, j, t, step):
        red, _, cz, ssem, _, csem = kind
        return remote(
            red.at[j, t], cz.at[j, t], ssem.at[j, t], csem.at[j, t],
            (row, (mz + step) * NX + mx),
        )

    def z_send(kind, j, t, dist, sign):
        if dist <= 2:
            z_near(kind, j, t, mz).start()
        else:
            z_chain(kind, j, t, sign).start()

    def z_first(kind, j):
        for dist in range(1, NZ):
            for sign in (1, -1):
                t = mz + sign * dist
                ready = inside(t)
                if dist > 1:
                    ready = jnp.logical_and(ready, outside(mz - sign))

                @pl.when(ready)
                def _():
                    z_send(kind, j, t, dist, sign)

    def z_between(kind, j):
        red, cz = kind[0], kind[2]
        for sign in (1, -1):
            for dist in range(2, NZ):
                t = mz + sign * dist

                @pl.when(jnp.logical_and(inside(t), inside(mz - sign)))
                def _():
                    z_chain(kind, j, t, -sign).wait_recv()
                    red[j, t] = (red[j, t].astype(F32) + cz[j, t].astype(F32)).astype(BF16)
                    z_send(kind, j, t, dist, sign)

    def z_last(kind, j, total):
        red, zr = kind[0], kind[1]
        total[...] = red[j, mz].astype(F32)
        for dist in (1, 2):
            for sign in (1, -1):
                src = mz + sign * dist

                @pl.when(inside(src))
                def _():
                    z_near(kind, j, src, src).wait_recv()
                    total[...] += zr[j, src].astype(F32)

    def a_sum(j, carry):
        for k in range(1, NX):
            xa_copy(j, xpeer(k), xpeer(k)).wait_recv()
        s = part_a[j, mx].astype(F32)
        for k in range(1, NX):
            s = s + xr_a[j, xpeer(k)].astype(F32)
        red_a[j] = s.astype(BF16)
        z_first(kinds[0], j)
        return carry

    lax.fori_loop(0, n, a_sum, 0)

    def agz_copy(j, src, dev):
        return remote(
            ag.at[j, mx, src], ag.at[j, mx, src], agz_s.at[j, dev], agz_r.at[j, src],
            (row, dev * NX + mx),
        )

    def agf_copy(j, src, dev):
        return remote(
            ag.at[j, mx, src], ag.at[j, mx, src], agf_s.at[j, src], agz_r.at[j, src],
            (row, dev * NX + mx),
        )

    def agx_copy(j, src, dev):
        return remote(
            ag.at[j, src], ag.at[j, src], agx_s.at[j, dev], agx_r.at[j, src],
            (row, mz * NX + dev),
        )

    def g_sum(j):
        for k in range(1, NX):
            xg_copy(j, xpeer(k), xpeer(k)).wait_recv()
        for z in range(NZ):
            s = part_g[j, mx, z].astype(F32)
            for k in range(1, NX):
                s = s + xr_g[j, xpeer(k), z].astype(F32)
            red_g[j, z] = s.astype(BF16)
        z_first(kinds[1], j)

    def between(j):
        for kind in kinds:
            z_between(kind, j)

    def pointwise(j):
        z_last(kinds[0], j, da_sum)
        z_last(kinds[1], j, gu_sum)
        da = da_sum[...]
        gate = gu_sum[0]
        up = gu_sum[1]
        sig = jax.nn.sigmoid(gate)
        ag[j, mx, mz, 0] = (gate * sig * up).astype(BF16)
        ag[j, mx, mz, 1] = (da * up * sig * (1.0 + gate * (1.0 - sig))).astype(BF16)
        ag[j, mx, mz, 2] = (da * gate * sig).astype(BF16)
        for dist in (1, 2):
            for sign in (1, -1):
                t = mz + sign * dist

                @pl.when(inside(t))
                def _():
                    agz_copy(j, mz, t).start()

    def pass_on(j, dists):
        for dist in dists:
            for sign in (1, -1):
                src = mz - sign * dist

                @pl.when(inside(src))
                def _():
                    agz_copy(j, src, src).wait_recv()

                if dist >= 2:

                    @pl.when(jnp.logical_and(inside(src), inside(mz + sign)))
                    def _():
                        agf_copy(j, src, mz + sign).start()

    def forward_x(j):
        pass_on(j, range(3, NZ))
        for k in range(1, NX):
            agx_copy(j, mx, xpeer(k)).start()

    def exchange(s, carry):
        stages = (
            g_sum, between, pointwise, lambda j: pass_on(j, range(1, min(3, NZ))), forward_x,
        )
        for depth, stage in enumerate(stages):

            @pl.when(jnp.logical_and(s >= depth, s < n + depth))
            def _():
                stage(s - depth)

        return carry

    lax.fori_loop(0, n + 4, exchange, 0)

    acc_d[...] = jnp.zeros_like(acc_d)
    acc_n[...] = jnp.zeros_like(acc_n)

    def products(j, carry):
        for k in range(1, NX):
            agx_copy(j, xpeer(k), xpeer(k)).wait_recv()
        cols = pl.ds(pl.multiple_of(j * width, width), width)

        def tokens(which):
            return jnp.concatenate(
                [ag[j, c % NX, c // NX, which] for c in range(C)], axis=0
            )

        act, gg, ug = tokens(0), tokens(1), tokens(2)
        act_all[:, cols] = act
        gg_all[:, cols] = gg
        ug_all[:, cols] = ug
        acc_d[...] += dot_nn(act, wd[cols, :])
        acc_n[...] += dot_nt(gg, wg[:, cols]) + dot_nt(ug, wu[:, cols])
        return carry

    lax.fori_loop(0, n, products, 0)

    for r in range(R):
        at = slice(r * rows, (r + 1) * rows)
        fin_s[r, 0] = acc_d[at, :].astype(BF16)
        fin_s[r, 1] = acc_n[at, :].astype(BF16)

    def fin_copy(src, dev):
        return remote(
            fin_s.at[dev], fin_r.at[src], fin_ss.at[dev], fin_rs.at[src], (dev, col)
        )

    for k in range(1, R):
        fin_copy(row, rpeer(k)).start()
    nm_out[...] = nm_all[...].reshape(R * rows, feats)
    og_out[...] = og_all[...].reshape(R * rows, feats)
    for k in range(1, R):
        fin_copy(rpeer(k), rpeer(k)).wait_recv()
    down = fin_s[row, 0].astype(F32)
    ngrad = fin_s[row, 1].astype(F32)
    for k in range(1, R):
        down = down + fin_r[rpeer(k), 0].astype(F32)
        ngrad = ngrad + fin_r[rpeer(k), 1].astype(F32)
    x = x_ref[...].astype(F32)
    dt_mine[...] = to_lanes(jnp.sum(ngrad * gain * x, axis=1, keepdims=True))
    gn_mine[...] = jnp.sum(ngrad * x * scale, axis=0, keepdims=True)

    def dt_copy(src, dev):
        return remote(dt_mine, dt_all.at[src], dt_s.at[dev], dt_r.at[src], (row, dev))

    def gn_copy(src, dev):
        return remote(gn_mine, gn_all.at[src], gn_s.at[dev], gn_r.at[src], (dev, col))

    for k in range(1, C):
        dt_copy(col, cpeer(k)).start()
    for k in range(1, R):
        gn_copy(row, rpeer(k)).start()
    dt_all[col] = dt_mine[...]
    gn_all[row] = gn_mine[...]
    out_ref[...] = (x + down).astype(BF16)
    for k in range(1, C):
        dt_copy(cpeer(k), cpeer(k)).wait_recv()
    dots = dt_all[0]
    for c in range(1, C):
        dots = dots + dt_all[c]
    dots = to_column(dots)
    ig_ref[...] = (
        og_ref[...].astype(F32)
        + scale * gain * ngrad
        - x * scale * scale * scale * dots / total_width
    ).astype(BF16)
    for k in range(1, R):
        gn_copy(rpeer(k), rpeer(k)).wait_recv()
    gain_sum = gn_all[0]
    for r in range(1, R):
        gain_sum = gain_sum + gn_all[r]
    gg_out[...] = gain_sum

    for k in range(1, R):
        og_copy(row, rpeer(k)).wait_send()
        nm_copy(row, rpeer(k)).wait_send()
        fin_copy(row, rpeer(k)).wait_send()
        gn_copy(row, rpeer(k)).wait_send()
    for k in range(1, C):
        sq_copy(col, cpeer(k)).wait_send()
        dt_copy(col, cpeer(k)).wait_send()

    def drain(j, carry):
        for k in range(1, NX):
            xa_copy(j, mx, xpeer(k)).wait_send()
            xg_copy(j, mx, xpeer(k)).wait_send()
            agx_copy(j, mx, xpeer(k)).wait_send()
        for k in range(1, NZ):
            for kind in kinds:
                z_near(kind, j, zpeer(k), mz).wait_send()
        for dist in range(1, NZ):
            for sign in (1, -1):
                t = mz + sign * dist
                if dist <= 2:

                    @pl.when(inside(t))
                    def _():
                        agz_copy(j, mz, t).wait_send()

                if dist >= 2:

                    @pl.when(jnp.logical_and(inside(t), inside(mz - sign)))
                    def _():
                        agf_copy(j, t, mz - sign).wait_send()

        return carry

    lax.fori_loop(0, n, drain, 0)


def wgrad_kernel(per, nm_ref, og_ref, act_ref, gg_ref, ug_ref, mg_ref, mu_ref, md_ref,
                 lo_ref, ig_ref, gn_ref, gw_ref, uw_ref, dw_ref, lo_out, ig_out, gn_out):
    @pl.when(pl.program_id(0) == 0)
    def _():
        lo_out[...] = lo_ref[...]
        ig_out[...] = ig_ref[...]
        gn_out[...] = gn_ref[...]

    feats = nm_ref.shape[1]
    for src, mask, dst in ((gg_ref, mg_ref, gw_ref), (ug_ref, mu_ref, uw_ref)):
        w = dot_tn(nm_ref[...], src[...])
        for r in range(feats // BLK):
            at = slice(r * BLK, (r + 1) * BLK)
            dst[at, :] = (w[at, :] * mask[r]).astype(BF16)
    w = dot_tn(act_ref[...], og_ref[...])
    for r in range(per):
        at = slice(r * BLK, (r + 1) * BLK)
        dw_ref[at, :] = (w[at, :] * md_ref[r]).astype(BF16)


def shards(R, C, layer_input, norm_gain, w_gate, w_up, w_down,
           mask_gate, mask_up, mask_down, out_grad):
    rows, feats = layer_input.shape
    hidden = w_gate.shape[1]
    tokens = rows * R
    T = tokens // C
    NX = 1
    while (2 * NX) * (2 * NX) <= C:
        NX *= 2
    NZ = C // NX
    width = chunk_width(hidden)
    n = hidden // width
    per = width // BLK
    wide_gate = jnp.repeat(mask_gate.astype(F32), BLK, axis=1)[:, None, :]
    wide_up = jnp.repeat(mask_up.astype(F32), BLK, axis=1)[:, None, :]
    wide_down = jnp.repeat(mask_down.astype(F32), BLK, axis=1)[:, None, :]
    vm = pl.BlockSpec(memory_space=pltpu.VMEM)
    hbm = pl.BlockSpec(memory_space=pl.ANY)
    dma = pltpu.SemaphoreType.DMA
    V = pltpu.VMEM
    out_shapes = (
        ((rows, feats), BF16), ((rows, feats), BF16), ((1, feats), F32),
        ((tokens, hidden), BF16), ((tokens, hidden), BF16), ((tokens, hidden), BF16),
        ((tokens, feats), BF16), ((tokens, feats), BF16),
    )
    scratch = [
        V((feats, hidden), BF16), V((feats, hidden), BF16), V((hidden, feats), BF16),
        V((R, rows, feats), BF16), V((R, rows, feats), BF16),
        V((1, LANES), F32), V((C, 1, LANES), F32),
        V((n, NX, NZ, T, width), BF16), V((n, NX, NZ, 2, T, width), BF16),
        V((n, NX, NZ, T, width), BF16), V((n, NX, NZ, 2, T, width), BF16),
        V((n, NZ, T, width), BF16), V((n, NZ, 2, T, width), BF16),
        V((n, NZ, T, width), BF16), V((n, NZ, 2, T, width), BF16),
        V((n, NZ, T, width), BF16), V((n, NZ, 2, T, width), BF16),
        V((T, width), F32), V((2, T, width), F32),
        V((n, NX, NZ, 3, T, width), BF16),
        V((tokens, feats), F32), V((tokens, feats), F32),
        V((R, 2, rows, feats), BF16), V((R, 2, rows, feats), BF16),
        V((1, feats), F32), V((R, 1, feats), F32),
        V((1, LANES), F32), V((C, 1, LANES), F32),
        dma((3,)),
        dma((R,)), dma((R,)), dma((R,)), dma((R,)), dma((C,)), dma((C,)),
        dma((n, NX)), dma((n, NX)), dma((n, NX)), dma((n, NX)),
        dma((n, NZ)), dma((n, NZ)), dma((n, NZ)), dma((n, NZ)), dma((n, NZ)), dma((n, NZ)),
        dma((n, NZ)), dma((n, NZ)), dma((n, NZ)), dma((n, NX)), dma((n, NX)),
        dma((R,)), dma((R,)), dma((R,)), dma((R,)), dma((C,)), dma((C,)),
        dma((1,)),
    ]
    layer_out, input_grad, gain_grad, act, gg, ug, nm, og = pl.pallas_call(
        functools.partial(layer_kernel, R, NZ, NX, width, float(feats * C)),
        out_shape=tuple(jax.ShapeDtypeStruct(s, t) for s, t in out_shapes),
        in_specs=[vm] * 6 + [hbm] * 3,
        out_specs=tuple([vm] * 8),
        scratch_shapes=scratch,
        compiler_params=pltpu.CompilerParams(
            collective_id=0, has_side_effects=True, vmem_limit_bytes=67043328
        ),
    )(layer_input, norm_gain[None, :], out_grad, wide_gate, wide_up, wide_down,
      w_gate, w_up, w_down)

    whole = lambda j: (0, 0)
    gate_wgrad, up_wgrad, down_wgrad, layer_out, input_grad, gain_grad = pl.pallas_call(
        functools.partial(wgrad_kernel, per),
        grid=(n,),
        out_shape=(
            jax.ShapeDtypeStruct((feats, hidden), BF16),
            jax.ShapeDtypeStruct((feats, hidden), BF16),
            jax.ShapeDtypeStruct((hidden, feats), BF16),
            jax.ShapeDtypeStruct((rows, feats), BF16),
            jax.ShapeDtypeStruct((rows, feats), BF16),
            jax.ShapeDtypeStruct((1, feats), F32),
        ),
        in_specs=[
            pl.BlockSpec((tokens, feats), whole),
            pl.BlockSpec((tokens, feats), whole),
            pl.BlockSpec((tokens, width), lambda j: (0, j)),
            pl.BlockSpec((tokens, width), lambda j: (0, j)),
            pl.BlockSpec((tokens, width), lambda j: (0, j)),
            pl.BlockSpec((feats // BLK, 1, width), lambda j: (0, 0, j)),
            pl.BlockSpec((feats // BLK, 1, width), lambda j: (0, 0, j)),
            pl.BlockSpec((per, 1, feats), lambda j: (j, 0, 0)),
            pl.BlockSpec((rows, feats), whole),
            pl.BlockSpec((rows, feats), whole),
            pl.BlockSpec((1, feats), whole),
        ],
        out_specs=(
            pl.BlockSpec((feats, width), lambda j: (0, j)),
            pl.BlockSpec((feats, width), lambda j: (0, j)),
            pl.BlockSpec((width, feats), lambda j: (j, 0)),
            pl.BlockSpec((rows, feats), whole),
            pl.BlockSpec((rows, feats), whole),
            pl.BlockSpec((1, feats), whole),
        ),
        compiler_params=pltpu.CompilerParams(vmem_limit_bytes=67043328),
    )(nm, og, act, gg, ug, wide_gate, wide_up, wide_down, layer_out, input_grad, gain_grad)
    return (layer_out, input_grad, gain_grad[0], gate_wgrad, up_wgrad, down_wgrad)


def solution(mesh):
    placed = (
        P("row", "col"),
        P("col"),
        P("col", "row"),
        P("col", "row"),
        P("row", "col"),
        P("col", "row"),
        P("col", "row"),
        P("row", "col"),
        P("row", "col"),
    )
    return jax.shard_map(
        functools.partial(shards, mesh.shape["row"], mesh.shape["col"]),
        mesh=mesh,
        in_specs=placed,
        out_specs=(
            P("row", "col"),
            P("row", "col"),
            P("col"),
            P("col", "row"),
            P("col", "row"),
            P("row", "col"),
        ),
        check_vma=False,
    )
```

```python
import functools

import jax
import jax.numpy as jnp
from jax import lax
from jax.experimental import pallas as pl
from jax.experimental.pallas import tpu as pltpu
from jax.sharding import PartitionSpec as P

BLK = 128
LANES = 128
MESH = pl.DeviceIdType.MESH
F32 = jnp.float32
BF16 = jnp.bfloat16
norm_eps = 1e-05


def dot_nn(left, right):
    return lax.dot_general(left, right, (((1,), (0,)), ((), ())), preferred_element_type=F32)


def dot_nt(left, right):
    return lax.dot_general(left, right, (((1,), (1,)), ((), ())), preferred_element_type=F32)


def dot_tn(left, right):
    return lax.dot_general(left, right, (((0,), (0,)), ((), ())), preferred_element_type=F32)


def chunk_width(hidden, widths):
    for width in widths:
        if hidden % width == 0:
            return width
    return hidden


def layer_kernel(
    R, NZ, NX, width, total_width,
    x_ref, gain_ref, og_ref, mg_ref, mu_ref, md_ref, wg_hbm, wu_hbm, wd_hbm,
    out_ref, ig_ref, gg_out, act_all, gg_all, ug_all, nm_out, og_out,
    wg, wu, wd, nm_all, og_all, sq_mine, sq_all, part_a, part_g, xr_a, xr_g,
    red_a, red_g, zr_a, zr_g, cz_a, cz_g, da_sum, gu_sum, ag, acc_d, acc_n, fin_s, fin_r, gn_mine, gn_all,
    dt_mine, dt_all,
    w_sem, og_s, og_r, nm_s, nm_r, sq_s, sq_r, xa_s, xa_r, xg_s, xg_r,
    za_s, za_r, zg_s, zg_r, ca_r, cg_r, agz_s, agz_r, agf_s, agx_s, agx_r, fin_ss, fin_rs,
    gn_s, gn_r, dt_s, dt_r, loc_s,
):
    C = NZ * NX
    row = lax.axis_index("row")
    col = lax.axis_index("col")
    mz = col // NX
    mx = lax.rem(col, NX)
    rows, feats = x_ref.shape
    hidden = wg.shape[1]
    n = hidden // width
    T = part_a.shape[3]
    per = width // BLK

    def rpeer(k):
        return lax.rem(row + k, R)

    def cpeer(k):
        return lax.rem(col + k, C)

    def xpeer(k):
        return lax.rem(mx + k, NX)

    def zpeer(k):
        return lax.rem(mz + k, NZ)

    def remote(src, dst, ssem, rsem, dev):
        return pltpu.make_async_remote_copy(
            src_ref=src, dst_ref=dst, send_sem=ssem, recv_sem=rsem,
            device_id=dev, device_id_type=MESH,
        )

    barrier = pltpu.get_barrier_semaphore()
    for k in range(1, R):
        pl.semaphore_signal(barrier, inc=1, device_id=(rpeer(k), col), device_id_type=MESH)
    for k in range(1, C):
        pl.semaphore_signal(barrier, inc=1, device_id=(row, cpeer(k)), device_id_type=MESH)
    loads = [
        pltpu.make_async_copy(src, dst, w_sem.at[i])
        for i, (src, dst) in enumerate(((wd_hbm, wd), (wg_hbm, wg), (wu_hbm, wu)))
    ]
    for load in loads:
        load.start()
    pl.semaphore_wait(barrier, R - 1 + C - 1)

    def og_copy(src, dev):
        return remote(og_ref, og_all.at[src], og_s.at[dev], og_r.at[src], (dev, col))

    for k in range(1, R):
        og_copy(row, rpeer(k)).start()
    own_og = pltpu.make_async_copy(og_ref, og_all.at[row], loc_s.at[0])
    own_og.start()

    x = x_ref[...].astype(F32)
    tok = lax.broadcasted_iota(jnp.int32, (rows, LANES), 0)
    lane = lax.broadcasted_iota(jnp.int32, (rows, LANES), 1)
    diag = tok == lane

    def to_lanes(column):
        return jnp.sum(jnp.where(diag, column, 0.0), axis=0, keepdims=True)

    def to_column(line):
        return jnp.sum(jnp.where(diag, line, 0.0), axis=1, keepdims=True)

    sq_mine[...] = to_lanes(jnp.sum(x * x, axis=1, keepdims=True))

    def sq_copy(src, dev):
        return remote(sq_mine, sq_all.at[src], sq_s.at[dev], sq_r.at[src], (row, dev))

    for k in range(1, C):
        sq_copy(col, cpeer(k)).start()

    loads[0].wait()
    own_og.wait()
    for k in range(1, R):
        og_copy(rpeer(k), rpeer(k)).wait_recv()

    def xa_copy(j, src, dev):
        return remote(
            part_a.at[j, dev], xr_a.at[j, src], xa_s.at[j, dev], xa_r.at[j, src],
            (row, mz * NX + dev),
        )

    def xg_copy(j, src, dev):
        return remote(
            part_g.at[j, dev], xr_g.at[j, src], xg_s.at[j, dev], xg_r.at[j, src],
            (row, mz * NX + dev),
        )

    def a_part(j, carry):
        base = pl.multiple_of(j * width, width)
        for r in range(per):
            at = pl.ds(pl.multiple_of(base + r * BLK, BLK), BLK)
            wd[at, :] = wd[at, :] * md_ref[j * per + r].astype(BF16)
        a = dot_nt(
            og_all[...].reshape(R * rows, feats), wd[pl.ds(base, width), :]
        ).astype(BF16)
        for z in range(NZ):
            for xx in range(NX):
                c = z * NX + xx
                part_a[j, xx, z] = a[c * T : (c + 1) * T]
        for k in range(1, NX):
            xa_copy(j, mx, xpeer(k)).start()
        return carry

    lax.fori_loop(0, n, a_part, 0)

    sq_all[col] = sq_mine[...]
    for k in range(1, C):
        sq_copy(cpeer(k), cpeer(k)).wait_recv()
    total = sq_all[0]
    for c in range(1, C):
        total = total + sq_all[c]
    scale = lax.rsqrt(to_column(total) / total_width + norm_eps)
    gain = gain_ref[...]
    nm_all[row] = (x * scale * gain).astype(BF16)

    def nm_copy(src, dev):
        return remote(
            nm_all.at[src], nm_all.at[src], nm_s.at[dev], nm_r.at[src], (dev, col)
        )

    for k in range(1, R):
        nm_copy(row, rpeer(k)).start()
    loads[1].wait()
    loads[2].wait()

    def mask_columns(j, carry):
        cols = pl.ds(pl.multiple_of(j * width, width), width)
        for r in range(feats // BLK):
            at = slice(r * BLK, (r + 1) * BLK)
            wg[at, cols] = wg[at, cols] * mg_ref[r, :, cols].astype(BF16)
            wu[at, cols] = wu[at, cols] * mu_ref[r, :, cols].astype(BF16)
        return carry

    lax.fori_loop(0, n, mask_columns, 0)
    for k in range(1, R):
        nm_copy(rpeer(k), rpeer(k)).wait_recv()

    def g_part(j, carry):
        cols = pl.ds(pl.multiple_of(j * width, width), width)
        nm = nm_all[...].reshape(R * rows, feats)
        for which, w in enumerate((wg, wu)):
            p = dot_nn(nm, w[:, cols]).astype(BF16)
            for z in range(NZ):
                for xx in range(NX):
                    c = z * NX + xx
                    part_g[j, xx, z, which] = p[c * T : (c + 1) * T]
        for k in range(1, NX):
            xg_copy(j, mx, xpeer(k)).start()
        return carry

    lax.fori_loop(0, n, g_part, 0)

    def inside(z):
        return jnp.logical_and(z >= 0, z < NZ)

    def outside(z):
        return jnp.logical_or(z < 0, z >= NZ)

    kinds = ((red_a, zr_a, cz_a, za_s, za_r, ca_r), (red_g, zr_g, cz_g, zg_s, zg_r, cg_r))

    def z_near(kind, j, t, src):
        red, zr, _, ssem, rsem, _ = kind
        return remote(
            red.at[j, t], zr.at[j, src], ssem.at[j, t], rsem.at[j, src], (row, t * NX + mx)
        )

    def z_chain(kind, j, t, step):
        red, _, cz, ssem, _, csem = kind
        return remote(
            red.at[j, t], cz.at[j, t], ssem.at[j, t], csem.at[j, t],
            (row, (mz + step) * NX + mx),
        )

    def z_send(kind, j, t, dist, sign):
        if dist <= 2:
            z_near(kind, j, t, mz).start()
        else:
            z_chain(kind, j, t, sign).start()

    def z_first(kind, j):
        for dist in range(1, NZ):
            for sign in (1, -1):
                t = mz + sign * dist
                ready = inside(t)
                if dist > 1:
                    ready = jnp.logical_and(ready, outside(mz - sign))

                @pl.when(ready)
                def _():
                    z_send(kind, j, t, dist, sign)

    def z_between(kind, j):
        red, cz = kind[0], kind[2]
        for sign in (1, -1):
            for dist in range(2, NZ):
                t = mz + sign * dist

                @pl.when(jnp.logical_and(inside(t), inside(mz - sign)))
                def _():
                    z_chain(kind, j, t, -sign).wait_recv()
                    red[j, t] = (red[j, t].astype(F32) + cz[j, t].astype(F32)).astype(BF16)
                    z_send(kind, j, t, dist, sign)

    def z_last(kind, j, total):
        red, zr = kind[0], kind[1]
        total[...] = red[j, mz].astype(F32)
        for dist in (1, 2):
            for sign in (1, -1):
                src = mz + sign * dist

                @pl.when(inside(src))
                def _():
                    z_near(kind, j, src, src).wait_recv()
                    total[...] += zr[j, src].astype(F32)

    def a_sum(j, carry):
        for k in range(1, NX):
            xa_copy(j, xpeer(k), xpeer(k)).wait_recv()
        s = part_a[j, mx].astype(F32)
        for k in range(1, NX):
            s = s + xr_a[j, xpeer(k)].astype(F32)
        red_a[j] = s.astype(BF16)
        z_first(kinds[0], j)
        return carry

    lax.fori_loop(0, n, a_sum, 0)

    def agz_copy(j, src, dev):
        return remote(
            ag.at[j, mx, src], ag.at[j, mx, src], agz_s.at[j, dev], agz_r.at[j, src],
            (row, dev * NX + mx),
        )

    def agf_copy(j, src, dev):
        return remote(
            ag.at[j, mx, src], ag.at[j, mx, src], agf_s.at[j, src], agz_r.at[j, src],
            (row, dev * NX + mx),
        )

    def agx_copy(j, src, dev):
        return remote(
            ag.at[j, src], ag.at[j, src], agx_s.at[j, dev], agx_r.at[j, src],
            (row, mz * NX + dev),
        )

    def g_sum(j):
        for k in range(1, NX):
            xg_copy(j, xpeer(k), xpeer(k)).wait_recv()
        for z in range(NZ):
            s = part_g[j, mx, z].astype(F32)
            for k in range(1, NX):
                s = s + xr_g[j, xpeer(k), z].astype(F32)
            red_g[j, z] = s.astype(BF16)
        z_first(kinds[1], j)

    def between(j):
        for kind in kinds:
            z_between(kind, j)

    def pointwise(j):
        z_last(kinds[0], j, da_sum)
        z_last(kinds[1], j, gu_sum)
        da = da_sum[...]
        gate = gu_sum[0]
        up = gu_sum[1]
        sig = jax.nn.sigmoid(gate)
        ag[j, mx, mz, 0] = (gate * sig * up).astype(BF16)
        ag[j, mx, mz, 1] = (da * up * sig * (1.0 + gate * (1.0 - sig))).astype(BF16)
        ag[j, mx, mz, 2] = (da * gate * sig).astype(BF16)
        for dist in (1, 2):
            for sign in (1, -1):
                t = mz + sign * dist

                @pl.when(inside(t))
                def _():
                    agz_copy(j, mz, t).start()

    def pass_on(j, dists):
        for dist in dists:
            for sign in (1, -1):
                src = mz - sign * dist

                @pl.when(inside(src))
                def _():
                    agz_copy(j, src, src).wait_recv()

                if dist >= 2:

                    @pl.when(jnp.logical_and(inside(src), inside(mz + sign)))
                    def _():
                        agf_copy(j, src, mz + sign).start()

    def forward_x(j):
        pass_on(j, range(3, NZ))
        for k in range(1, NX):
            agx_copy(j, mx, xpeer(k)).start()

    def exchange(s, carry):
        stages = (
            g_sum, between, pointwise, lambda j: pass_on(j, range(1, min(3, NZ))), forward_x,
        )
        for depth, stage in enumerate(stages):

            @pl.when(jnp.logical_and(s >= depth, s < n + depth))
            def _():
                stage(s - depth)

        return carry

    lax.fori_loop(0, n + 4, exchange, 0)

    acc_d[...] = jnp.zeros_like(acc_d)
    acc_n[...] = jnp.zeros_like(acc_n)

    def products(j, carry):
        for k in range(1, NX):
            agx_copy(j, xpeer(k), xpeer(k)).wait_recv()
        cols = pl.ds(pl.multiple_of(j * width, width), width)

        def tokens(which):
            return jnp.concatenate(
                [ag[j, c % NX, c // NX, which] for c in range(C)], axis=0
            )

        act, gg, ug = tokens(0), tokens(1), tokens(2)
        act_all[:, cols] = act
        gg_all[:, cols] = gg
        ug_all[:, cols] = ug
        acc_d[...] += dot_nn(act, wd[cols, :])
        acc_n[...] += dot_nt(gg, wg[:, cols]) + dot_nt(ug, wu[:, cols])
        return carry

    lax.fori_loop(0, n, products, 0)

    for r in range(R):
        at = slice(r * rows, (r + 1) * rows)
        fin_s[r, 0] = acc_d[at, :].astype(BF16)
        fin_s[r, 1] = acc_n[at, :].astype(BF16)

    def fin_copy(src, dev):
        return remote(
            fin_s.at[dev], fin_r.at[src], fin_ss.at[dev], fin_rs.at[src], (dev, col)
        )

    for k in range(1, R):
        fin_copy(row, rpeer(k)).start()
    nm_out[...] = nm_all[...].reshape(R * rows, feats)
    og_out[...] = og_all[...].reshape(R * rows, feats)
    for k in range(1, R):
        fin_copy(rpeer(k), rpeer(k)).wait_recv()
    down = fin_s[row, 0].astype(F32)
    ngrad = fin_s[row, 1].astype(F32)
    for k in range(1, R):
        down = down + fin_r[rpeer(k), 0].astype(F32)
        ngrad = ngrad + fin_r[rpeer(k), 1].astype(F32)
    x = x_ref[...].astype(F32)
    dt_mine[...] = to_lanes(jnp.sum(ngrad * gain * x, axis=1, keepdims=True))
    gn_mine[...] = jnp.sum(ngrad * x * scale, axis=0, keepdims=True)

    def dt_copy(src, dev):
        return remote(dt_mine, dt_all.at[src], dt_s.at[dev], dt_r.at[src], (row, dev))

    def gn_copy(src, dev):
        return remote(gn_mine, gn_all.at[src], gn_s.at[dev], gn_r.at[src], (dev, col))

    for k in range(1, C):
        dt_copy(col, cpeer(k)).start()
    for k in range(1, R):
        gn_copy(row, rpeer(k)).start()
    dt_all[col] = dt_mine[...]
    gn_all[row] = gn_mine[...]
    out_ref[...] = (x + down).astype(BF16)
    for k in range(1, C):
        dt_copy(cpeer(k), cpeer(k)).wait_recv()
    dots = dt_all[0]
    for c in range(1, C):
        dots = dots + dt_all[c]
    dots = to_column(dots)
    ig_ref[...] = (
        og_ref[...].astype(F32)
        + scale * gain * ngrad
        - x * scale * scale * scale * dots / total_width
    ).astype(BF16)
    for k in range(1, R):
        gn_copy(rpeer(k), rpeer(k)).wait_recv()
    gain_sum = gn_all[0]
    for r in range(1, R):
        gain_sum = gain_sum + gn_all[r]
    gg_out[...] = gain_sum

    for k in range(1, R):
        og_copy(row, rpeer(k)).wait_send()
        nm_copy(row, rpeer(k)).wait_send()
        fin_copy(row, rpeer(k)).wait_send()
        gn_copy(row, rpeer(k)).wait_send()
    for k in range(1, C):
        sq_copy(col, cpeer(k)).wait_send()
        dt_copy(col, cpeer(k)).wait_send()

    def drain(j, carry):
        for k in range(1, NX):
            xa_copy(j, mx, xpeer(k)).wait_send()
            xg_copy(j, mx, xpeer(k)).wait_send()
            agx_copy(j, mx, xpeer(k)).wait_send()
        for k in range(1, NZ):
            for kind in kinds:
                z_near(kind, j, zpeer(k), mz).wait_send()
        for dist in range(1, NZ):
            for sign in (1, -1):
                t = mz + sign * dist
                if dist <= 2:

                    @pl.when(inside(t))
                    def _():
                        agz_copy(j, mz, t).wait_send()

                if dist >= 2:

                    @pl.when(jnp.logical_and(inside(t), inside(mz - sign)))
                    def _():
                        agf_copy(j, t, mz - sign).wait_send()

        return carry

    lax.fori_loop(0, n, drain, 0)


def wgrad_kernel(per, nm_ref, og_ref, act_ref, gg_ref, ug_ref, mg_ref, mu_ref, md_ref,
                 lo_ref, ig_ref, gn_ref, gw_ref, uw_ref, dw_ref, lo_out, ig_out, gn_out):
    @pl.when(pl.program_id(0) == 0)
    def _():
        lo_out[...] = lo_ref[...]
        ig_out[...] = ig_ref[...]
        gn_out[...] = gn_ref[...]

    feats = nm_ref.shape[1]
    for src, mask, dst in ((gg_ref, mg_ref, gw_ref), (ug_ref, mu_ref, uw_ref)):
        w = dot_tn(nm_ref[...], src[...])
        for r in range(feats // BLK):
            at = slice(r * BLK, (r + 1) * BLK)
            dst[at, :] = (w[at, :] * mask[r]).astype(BF16)
    w = dot_tn(act_ref[...], og_ref[...])
    for r in range(per):
        at = slice(r * BLK, (r + 1) * BLK)
        dw_ref[at, :] = (w[at, :] * md_ref[r]).astype(BF16)


def shards(R, C, layer_input, norm_gain, w_gate, w_up, w_down,
           mask_gate, mask_up, mask_down, out_grad):
    rows, feats = layer_input.shape
    hidden = w_gate.shape[1]
    tokens = rows * R
    T = tokens // C
    NX = 1
    while (2 * NX) * (2 * NX) <= C:
        NX *= 2
    NZ = C // NX
    width = chunk_width(hidden, (256, 128))
    n = hidden // width
    per = width // BLK
    wide_gate = jnp.repeat(mask_gate.astype(F32), BLK, axis=1)[:, None, :]
    wide_up = jnp.repeat(mask_up.astype(F32), BLK, axis=1)[:, None, :]
    wide_down = jnp.repeat(mask_down.astype(F32), BLK, axis=1)[:, None, :]
    vm = pl.BlockSpec(memory_space=pltpu.VMEM)
    hbm = pl.BlockSpec(memory_space=pl.ANY)
    dma = pltpu.SemaphoreType.DMA
    V = pltpu.VMEM
    out_shapes = (
        ((rows, feats), BF16), ((rows, feats), BF16), ((1, feats), F32),
        ((tokens, hidden), BF16), ((tokens, hidden), BF16), ((tokens, hidden), BF16),
        ((tokens, feats), BF16), ((tokens, feats), BF16),
    )
    scratch = [
        V((feats, hidden), BF16), V((feats, hidden), BF16), V((hidden, feats), BF16),
        V((R, rows, feats), BF16), V((R, rows, feats), BF16),
        V((1, LANES), F32), V((C, 1, LANES), F32),
        V((n, NX, NZ, T, width), BF16), V((n, NX, NZ, 2, T, width), BF16),
        V((n, NX, NZ, T, width), BF16), V((n, NX, NZ, 2, T, width), BF16),
        V((n, NZ, T, width), BF16), V((n, NZ, 2, T, width), BF16),
        V((n, NZ, T, width), BF16), V((n, NZ, 2, T, width), BF16),
        V((n, NZ, T, width), BF16), V((n, NZ, 2, T, width), BF16),
        V((T, width), F32), V((2, T, width), F32),
        V((n, NX, NZ, 3, T, width), BF16),
        V((tokens, feats), F32), V((tokens, feats), F32),
        V((R, 2, rows, feats), BF16), V((R, 2, rows, feats), BF16),
        V((1, feats), F32), V((R, 1, feats), F32),
        V((1, LANES), F32), V((C, 1, LANES), F32),
        dma((3,)),
        dma((R,)), dma((R,)), dma((R,)), dma((R,)), dma((C,)), dma((C,)),
        dma((n, NX)), dma((n, NX)), dma((n, NX)), dma((n, NX)),
        dma((n, NZ)), dma((n, NZ)), dma((n, NZ)), dma((n, NZ)), dma((n, NZ)), dma((n, NZ)),
        dma((n, NZ)), dma((n, NZ)), dma((n, NZ)), dma((n, NX)), dma((n, NX)),
        dma((R,)), dma((R,)), dma((R,)), dma((R,)), dma((C,)), dma((C,)),
        dma((1,)),
    ]
    layer_out, input_grad, gain_grad, act, gg, ug, nm, og = pl.pallas_call(
        functools.partial(layer_kernel, R, NZ, NX, width, float(feats * C)),
        out_shape=tuple(jax.ShapeDtypeStruct(s, t) for s, t in out_shapes),
        in_specs=[vm] * 6 + [hbm] * 3,
        out_specs=tuple([vm] * 8),
        scratch_shapes=scratch,
        compiler_params=pltpu.CompilerParams(
            collective_id=0, has_side_effects=True, vmem_limit_bytes=67043328
        ),
    )(layer_input, norm_gain[None, :], out_grad, wide_gate, wide_up, wide_down,
      w_gate, w_up, w_down)

    width = chunk_width(hidden, (512, 256, 128))
    n = hidden // width
    per = width // BLK
    whole = lambda j: (0, 0)
    gate_wgrad, up_wgrad, down_wgrad, layer_out, input_grad, gain_grad = pl.pallas_call(
        functools.partial(wgrad_kernel, per),
        grid=(n,),
        out_shape=(
            jax.ShapeDtypeStruct((feats, hidden), BF16),
            jax.ShapeDtypeStruct((feats, hidden), BF16),
            jax.ShapeDtypeStruct((hidden, feats), BF16),
            jax.ShapeDtypeStruct((rows, feats), BF16),
            jax.ShapeDtypeStruct((rows, feats), BF16),
            jax.ShapeDtypeStruct((1, feats), F32),
        ),
        in_specs=[
            pl.BlockSpec((tokens, feats), whole),
            pl.BlockSpec((tokens, feats), whole),
            pl.BlockSpec((tokens, width), lambda j: (0, j)),
            pl.BlockSpec((tokens, width), lambda j: (0, j)),
            pl.BlockSpec((tokens, width), lambda j: (0, j)),
            pl.BlockSpec((feats // BLK, 1, width), lambda j: (0, 0, j)),
            pl.BlockSpec((feats // BLK, 1, width), lambda j: (0, 0, j)),
            pl.BlockSpec((per, 1, feats), lambda j: (j, 0, 0)),
            pl.BlockSpec((rows, feats), whole),
            pl.BlockSpec((rows, feats), whole),
            pl.BlockSpec((1, feats), whole),
        ],
        out_specs=(
            pl.BlockSpec((feats, width), lambda j: (0, j)),
            pl.BlockSpec((feats, width), lambda j: (0, j)),
            pl.BlockSpec((width, feats), lambda j: (j, 0)),
            pl.BlockSpec((rows, feats), whole),
            pl.BlockSpec((rows, feats), whole),
            pl.BlockSpec((1, feats), whole),
        ),
        compiler_params=pltpu.CompilerParams(vmem_limit_bytes=67043328),
    )(nm, og, act, gg, ug, wide_gate, wide_up, wide_down, layer_out, input_grad, gain_grad)
    return (layer_out, input_grad, gain_grad[0], gate_wgrad, up_wgrad, down_wgrad)


def solution(mesh):
    placed = (
        P("row", "col"),
        P("col"),
        P("col", "row"),
        P("col", "row"),
        P("row", "col"),
        P("col", "row"),
        P("col", "row"),
        P("row", "col"),
        P("row", "col"),
    )
    return jax.shard_map(
        functools.partial(shards, mesh.shape["row"], mesh.shape["col"]),
        mesh=mesh,
        in_specs=placed,
        out_specs=(
            P("row", "col"),
            P("row", "col"),
            P("col"),
            P("col", "row"),
            P("col", "row"),
            P("row", "col"),
        ),
        check_vma=False,
    )
```
